32 devices in a mesh: shard: 4 (over y, core), rep: 8 (over z, x).
Axes of the slice: x: 2, y: 2, z: 4, core: 2. Of those that a mesh axis runs over, the one named last changes fastest.
Arguments:
- block_input: bfloat16 [4096, 1024], P(('shard', 'rep')), may hold values from -6 to 6
- segments: int32 [4096], P(('shard', 'rep')), may hold values from 0 to 95, never falling along the last dimension, each value on 1 to 96 neighbouring positions
- cotangent: bfloat16 [4096, 1024], P(('shard', 'rep')), may hold values from -6 to 6
- gain_in: float32 [1024], replicated, may hold values from 0.5 to 1.5
- w_query: bfloat16 [1024, 768], P('shard'), may hold values from -0.1875 to 0.1875
- w_key: bfloat16 [1024, 768], P('shard'), may hold values from -0.1875 to 0.1875
- w_value: bfloat16 [1024, 1536], P('shard'), may hold values from -0.1875 to 0.1875
- conv_q: float32 [4, 768], replicated, may hold values from -3 to 3
- conv_k: float32 [4, 768], replicated, may hold values from -3 to 3
- conv_v: float32 [4, 1536], replicated, may hold values from -3 to 3
- w_decay: bfloat16 [1024, 6], replicated, may hold values from -0.1875 to 0.1875
- w_beta: bfloat16 [1024, 6], replicated, may hold values from -0.1875 to 0.1875
- a_log: float32 [6], replicated, may hold values from -3 to 0.5
- dt_bias: float32 [6], replicated, may hold values from -3 to -1
- w_gate_out: bfloat16 [1024, 1536], P('shard'), may hold values from -0.1875 to 0.1875
- gain_o: float32 [256], replicated, may hold values from 0.5 to 1.5
- w_out: bfloat16 [1536, 1024], P('shard'), may hold values from -0.3125 to 0.3125
- gain_mid: float32 [1024], replicated, may hold values from 0.5 to 1.5
- w_ffgate: bfloat16 [1024, 2816], P('shard'), may hold values from -0.1875 to 0.1875
- w_ffup: bfloat16 [1024, 2816], P('shard'), may hold values from -0.1875 to 0.1875
- w_down: bfloat16 [2816, 1024], P('shard'), may hold values from -0.21875 to 0.21875
Outputs:
- block_output: bfloat16 [4096, 1024], P(('shard', 'rep'))
- d_input: float32 [4096, 1024], P(('shard', 'rep'))
- d_gain_in: float32 [1024], replicated
- d_query: float32 [1024, 768], P('shard', 'rep')
- d_key: float32 [1024, 768], P('shard', 'rep')
- d_value: float32 [1024, 1536], P('shard', 'rep')
- d_conv_q: float32 [4, 768], replicated
- d_conv_k: float32 [4, 768], replicated
- d_conv_v: float32 [4, 1536], replicated
- d_decay: float32 [1024, 6], replicated
- d_beta: float32 [1024, 6], replicated
- d_a_log: float32 [6], replicated
- d_dt_bias: float32 [6], replicated
- d_gate_out: float32 [1024, 1536], P('shard', 'rep')
- d_gain_o: float32 [256], replicated
- d_out: float32 [1536, 1024], P('shard', 'rep')
- d_gain_mid: float32 [1024], replicated
- d_ffgate: float32 [1024, 2816], P('shard', 'rep')
- d_ffup: float32 [1024, 2816], P('shard', 'rep')
- d_down: float32 [2816, 1024], P('shard', 'rep')
The draws below stay inside these ranges and needn't reach their ends.
Inputs may be any that keep to these rules, and one draw needn't show every extreme that they name: `segments`: document numbers never fall along the tokens; a document covers 1 to (96) tokens, and one covers exactly that many.
All inputs are finite; a program needn't handle non-finite values.
Results may differ from the reference program's by a relative error of at most 0.017.
The reference program's roundings to bfloat16 on the way (of `normed`, `mixed`, `normed2`, `act` and `d_hidden_b`) count: a program that leaves them out, or rounds other values in their place, can miss the bound.
Values may be sent and summed in bfloat16 or wider, within the bound.
No kernel may reach another device: no remote copies, remote signals or barrier semaphores. Data moves between devices by JAX's collectives and lax.ppermute only.
A program may use at most 192 MiB of HBM per device.

```python
import math
from functools import partial
import jax
import jax.numpy as jnp
import numpy as np
from jax import lax

D = 1024
H = 6
DVH = 256
FF = 2816
CONV = 4
SPAN = 64
SEQ = 128
DK = 768
DV = 1536
TOKENS = 4096


def with_spikes(values, own_key, source, target, shards_of, factor):
    def block_of(axis_at):
        return (jnp.arange(values.shape[axis_at]) // (values.shape[axis_at] // shards_of)).reshape((-1,) + (1,) * (values.ndim - 1 - axis_at))

    near = jax.random.permutation(own_key, shards_of)[block_of(target)]
    second = (block_of(target) + shards_of // 2) % shards_of
    return jnp.where((block_of(source) == near) | (block_of(source) == second), factor * values, values)


def levels(key, shape, pieces, least, high):
    def one(dim, blocks):
        steps = jax.random.uniform(jax.random.fold_in(jax.random.fold_in(key, 6), dim), (blocks,), jnp.float32, least / len(pieces), high / len(pieces))
        return jnp.repeat(jnp.exp(steps), shape[dim] // blocks).reshape((-1,) + (1,) * (len(shape) - dim - 1))

    factor_of = one(*pieces[0])
    for cut in pieces[1:]:
        factor_of = factor_of * one(*cut)
    return factor_of


def profile(amount, total, bound, lean):
    loads = [(1 << 20) // math.isqrt(standing ** lean) + 1 for standing in range(2, amount + 1)]
    spare, holding = total - bound - (amount - 1), [1] * (amount - 1)
    while spare > 0:
        candidates = [i for i in range(amount - 1) if holding[i] < bound]
        whole, remaining = sum([loads[i] for i in candidates]), spare
        for i in candidates:
            addition = min(bound - holding[i], max(1, remaining * loads[i] // whole), spare)
            holding[i] = holding[i] + addition
            spare = spare - addition
    return np.array([bound] + holding)


def uneven(stream_key, number_of, total, bound, skew):
    if number_of == 2:
        one = jax.random.randint(stream_key, (), max(1, total - bound), min(bound, total - 1) + 1)
        return jnp.stack([one, total - one])
    sizes = jnp.asarray(profile(number_of, total, bound, skew), jnp.int32)
    pairs = (number_of - 1) // 2
    donor, receiver = sizes[1:1 + 2 * pairs:2], sizes[2:2 + 2 * pairs:2]
    margin = jnp.minimum(donor - 1, bound - receiver)
    moved = jax.random.randint(jax.random.fold_in(stream_key, 1), (pairs,), 0, 1 << 20) % (margin + 1)
    sizes = sizes.at[1:1 + 2 * pairs:2].set(donor - moved).at[2:2 + 2 * pairs:2].set(receiver + moved)
    return sizes[jax.random.permutation(jax.random.fold_in(stream_key, 2), number_of)]


def scatter_about(own_key, extent, scale, most, cuts=(), held_as=jnp.bfloat16):
    loudness = levels(own_key, extent, cuts, -0.22, 0.18) if cuts else 1.0
    entries = jax.random.normal(own_key, extent, jnp.float32) * scale * loudness
    return jnp.minimum(jnp.maximum(entries, -most), most).astype(held_as)


def bell_draw_with(rng, extent, spread, most, cuts, heavy, held_as=jnp.bfloat16):
    values = spread * jax.random.normal(rng, extent, jnp.float32)
    if cuts:
        values = values * levels(rng, extent, cuts, -0.22, 0.18)
    return jnp.clip(with_spikes(values, jax.random.fold_in(rng, 3), *heavy), -most, most).astype(held_as)


def setup_inputs(seed: int = 0) -> dict:
    seeds = jax.random.split(jax.random.key(seed), 22)
    return {
        "block_input": scatter_about(seeds[0], (TOKENS, D), 1.0, 6.0, ((0, 32),)),
        "segments": jnp.searchsorted(jnp.cumsum(uneven(seeds[1], 3 * TOKENS // SEQ, TOKENS, 3 * SEQ // 4, 2)), jnp.arange(TOKENS), side="right").astype(jnp.int32),
        "cotangent": bell_draw_with(seeds[2], (TOKENS, D), 1.0, 6.0, ((0, 32),), (0, 1, 32, 2.75)),
        "gain_in": jnp.clip(1.0 + 0.1 * jax.random.normal(seeds[3], (D,), jnp.float32), 0.5, 1.5),
        "w_query": scatter_about(seeds[4], (D, DK), D ** -0.5, 0.1875, ((0, 4),)),
        "w_key": scatter_about(seeds[5], (D, DK), D ** -0.5, 0.1875, ((0, 4),)),
        "w_value": scatter_about(seeds[6], (D, DV), D ** -0.5, 0.1875, ((0, 4),)),
        "conv_q": scatter_about(seeds[7], (CONV, DK), 0.5, 3.0, (), jnp.float32),
        "conv_k": scatter_about(seeds[8], (CONV, DK), 0.5, 3.0, (), jnp.float32),
        "conv_v": scatter_about(seeds[9], (CONV, DV), 0.5, 3.0, (), jnp.float32),
        "w_decay": scatter_about(seeds[10], (D, H), D ** -0.5, 0.1875),
        "w_beta": scatter_about(seeds[11], (D, H), D ** -0.5, 0.1875),
        "a_log": jnp.clip(jax.random.uniform(seeds[12], (H,), jnp.float32, -3.0, 0.5), -3.0, 0.5),
        "dt_bias": jnp.clip(jax.random.uniform(seeds[13], (H,), jnp.float32, -3.0, -1.0), -3.0, -1.0),
        "w_gate_out": scatter_about(seeds[14], (D, DV), D ** -0.5, 0.1875, ((0, 4),)),
        "gain_o": jnp.clip(1.0 + 0.1 * jax.random.normal(seeds[15], (DVH,), jnp.float32), 0.5, 1.5),
        "w_out": scatter_about(seeds[16], (DV, D), (DV // 4) ** -0.5, 0.3125, ((0, 4),)),
        "gain_mid": jnp.clip(1.0 + 0.1 * jax.random.normal(seeds[17], (D,), jnp.float32), 0.5, 1.5),
        "w_ffgate": scatter_about(seeds[18], (D, FF), D ** -0.5, 0.1875, ((0, 4),)),
        "w_ffup": scatter_about(seeds[19], (D, FF), D ** -0.5, 0.1875, ((0, 4),)),
        "w_down": scatter_about(seeds[20], (FF, D), (FF // 4) ** -0.5, 0.21875, ((0, 4),)),
    }


def norm_apply(hidden, gain):
    return hidden * lax.rsqrt(lax.optimization_barrier(jnp.mean(hidden * hidden, axis=-1, keepdims=True)) + 1e-05) * gain

def causal_conv(stream, taps, same_list):
    total = stream * taps[0]
    for lag in range(1, taps.shape[0]):
        moved = jnp.pad(stream, ((0, 0), (lag, 0), (0, 0)))[:, :stream.shape[1]]
        total = total + moved * taps[lag] * same_list[lag][:, :, None]
    return jax.nn.silu(total)

def unit_heads(stream, heads):
    batch, length, width = stream.shape
    split = stream.reshape(batch, length, heads, width // heads)
    return split * lax.rsqrt(lax.optimization_barrier(jnp.sum(split * split, axis=-1, keepdims=True)) + 1e-06)

def to_blocks(array, batch, blocks):
    shaped = array.reshape((batch, blocks, SPAN) + array.shape[2:])
    return jnp.moveaxis(jnp.moveaxis(shaped, 1, 0), 2, 3)

def mixer(seg, qp, kp, vp, zp, decay_raw, beta_raw, conv_q, conv_k, conv_v, a_log, dt_bias, gain_o):
    batch, length = seg.shape
    heads = a_log.shape[0]
    highest = lax.Precision.HIGHEST
    same_list = []
    for lag in range(conv_q.shape[0]):
        earlier = jnp.pad(seg, ((0, 0), (lag, 0)), constant_values=-1)[:, :length]
        same_list.append((earlier == seg).astype(jnp.float32))
    query = unit_heads(causal_conv(qp, conv_q, same_list), heads)
    query = query * query.shape[-1] ** (-0.5)
    keys = unit_heads(causal_conv(kp, conv_k, same_list), heads)
    value = causal_conv(vp, conv_v, same_list)
    value = value.reshape(batch, length, heads, value.shape[-1] // heads)
    log_decay = -jnp.exp(a_log) * jax.nn.softplus(decay_raw + dt_bias)
    beta = jax.nn.sigmoid(beta_raw)
    blocks = length // SPAN
    query_b = to_blocks(query, batch, blocks)
    keys_b = to_blocks(keys, batch, blocks)
    value_b = to_blocks(value, batch, blocks)
    decay_b = to_blocks(log_decay, batch, blocks)
    beta_b = to_blocks(beta, batch, blocks)
    seg_b = jnp.moveaxis(seg.reshape(batch, blocks, SPAN), 1, 0)
    seg_prev = jnp.concatenate([jnp.full((1, batch), -1, seg.dtype), seg_b[:-1, :, -1]], axis=0)
    identity = jnp.eye(SPAN, dtype=jnp.float32)
    lower = jnp.tril(jnp.ones((SPAN, SPAN), jnp.float32))
    width_v = value.shape[-1]

    def span_step(state, items):
        qc, kc, vc, gc, bc, sc, sp = items
        cum = jnp.cumsum(gc, axis=-1)
        same = (sc[:, :, None] == sc[:, None, :]).astype(jnp.float32) * lower
        decay = jnp.exp(jnp.minimum(cum[..., :, None] - cum[..., None, :], 0.0)) * same[:, None]
        enter = jnp.exp(cum) * (sc == sp[:, None]).astype(jnp.float32)[:, None, :]
        inner = jnp.einsum('bhtd,bhsd->bhts', kc, kc, precision=highest)
        system = identity + bc[..., :, None] * decay * (1.0 - identity) * inner
        rhs = jnp.concatenate([bc[..., None] * vc, (bc * enter)[..., None] * kc], axis=-1)
        solved = jax.scipy.linalg.solve_triangular(system, rhs, lower=True, unit_diagonal=True)
        fresh = solved[..., :width_v] - jnp.einsum('bhtk,bhkv->bhtv', solved[..., width_v:], state, precision=highest)
        scores = jnp.einsum('bhtd,bhsd->bhts', qc, kc, precision=highest) * decay
        result = enter[..., None] * jnp.einsum('bhtk,bhkv->bhtv', qc, state, precision=highest)
        result = result + jnp.einsum('bhts,bhsv->bhtv', scores, fresh, precision=highest)
        weighted = decay[..., -1, :][..., None] * kc
        new_state = enter[..., -1][..., None, None] * state + jnp.einsum('bhsk,bhsv->bhkv', weighted, fresh, precision=highest)
        return (new_state, result)
    start = jnp.zeros((batch, heads, keys.shape[-1], width_v), jnp.float32)
    _, outs = lax.scan(span_step, start, (query_b, keys_b, value_b, decay_b, beta_b, seg_b, seg_prev))
    core = jnp.moveaxis(jnp.moveaxis(outs, 3, 2), 0, 1).reshape(batch, length, heads, width_v)
    gated = core * lax.rsqrt(lax.optimization_barrier(jnp.mean(core * core, axis=-1, keepdims=True)) + 1e-05) * gain_o
    gated = gated * jax.nn.silu(zp.reshape(batch, length, heads, width_v))
    return gated.reshape(batch, length, heads * width_v)

def dot_plain(left, right):
    return jnp.dot(left.astype(jnp.float32), right.astype(jnp.float32), preferred_element_type=jnp.float32)

def dot_trans(left, right):
    return lax.dot_general(left.astype(jnp.float32), right.astype(jnp.float32), (((1,), (1,)), ((), ())), preferred_element_type=jnp.float32)

def dot_outer(left, right):
    return lax.dot_general(left.astype(jnp.float32), right.astype(jnp.float32), (((0,), (0,)), ((), ())), preferred_element_type=jnp.float32)

def forward_pass(tokens_in, segments, large, small):
    w_query, w_key, w_value, w_gate_out, w_out, w_ffgate, w_ffup, w_down = large
    gain_in, gain_mid, conv_q, conv_k, conv_v, w_decay, w_beta, a_log, dt_bias, gain_o = small
    rows = tokens_in.shape[0]
    batch = rows // SEQ
    seg = segments.reshape(batch, SEQ)
    resid = tokens_in.astype(jnp.float32)
    normed = norm_apply(resid, gain_in).astype(jnp.bfloat16)
    inputs = tuple((dot_plain(normed, weight) for weight in (w_query, w_key, w_value, w_gate_out, w_decay, w_beta)))
    shaped = tuple((item.reshape(batch, SEQ, item.shape[-1]) for item in inputs))
    mixed = mixer(seg, *shaped, conv_q, conv_k, conv_v, a_log, dt_bias, gain_o).reshape(rows, -1).astype(jnp.bfloat16)
    hidden1 = resid + dot_plain(mixed, w_out)
    normed2 = norm_apply(hidden1, gain_mid).astype(jnp.bfloat16)
    gate = dot_plain(normed2, w_ffgate)
    up = dot_plain(normed2, w_ffup)
    act = (jax.nn.silu(gate) * up).astype(jnp.bfloat16)
    output = (hidden1 + dot_plain(act, w_down)).astype(jnp.bfloat16)
    saved = (resid, normed, shaped, seg, mixed, hidden1, normed2, gate, up, act)
    return (saved, output)

def backward_ffn(saved, cotangent, large, small):
    resid, normed, shaped, seg, mixed, hidden1, normed2, gate, up, act = saved
    w_ffgate, w_ffup, w_down = (large[5], large[6], large[7])
    gain_mid = small[1]
    g_down = dot_outer(act, cotangent)
    d_act = dot_trans(cotangent, w_down)
    sig = jax.nn.sigmoid(gate)
    d_gate = (d_act * up * sig * (1.0 + gate * (1.0 - sig))).astype(jnp.bfloat16)
    d_up = (d_act * gate * sig).astype(jnp.bfloat16)
    g_ffgate = dot_outer(normed2, d_gate)
    g_ffup = dot_outer(normed2, d_up)
    d_normed2 = dot_trans(d_gate, w_ffgate) + dot_trans(d_up, w_ffup)
    _, pull = jax.vjp(norm_apply, hidden1, gain_mid)
    d_from_norm, g_gain_mid = pull(d_normed2)
    d_hidden1 = cotangent.astype(jnp.float32) + d_from_norm
    return (d_hidden1, (g_ffgate, g_ffup, g_down), g_gain_mid)

def backward_mixer(saved, d_hidden1, large, small):
    resid, normed, shaped, seg, mixed, hidden1, normed2, gate, up, act = saved
    w_query, w_key, w_value, w_gate_out, w_out = large[:5]
    gain_in, gain_mid, conv_q, conv_k, conv_v, w_decay, w_beta, a_log, dt_bias, gain_o = small
    rows = resid.shape[0]
    d_hidden_b = d_hidden1.astype(jnp.bfloat16)
    g_out = dot_outer(mixed, d_hidden_b)
    d_mixed = dot_trans(d_hidden_b, w_out)
    _, pull = jax.vjp(partial(mixer, seg), *shaped, conv_q, conv_k, conv_v, a_log, dt_bias, gain_o)
    grads = pull(d_mixed.reshape(shaped[2].shape[0], SEQ, -1))
    flat = tuple((item.reshape(rows, -1).astype(jnp.bfloat16) for item in grads[:6]))
    weights = (w_query, w_key, w_value, w_gate_out, w_decay, w_beta)
    g_proj = tuple((dot_outer(normed, item) for item in flat))
    d_normed = dot_trans(flat[0], weights[0])
    for item, weight in zip(flat[1:], weights[1:]):
        d_normed = d_normed + dot_trans(item, weight)
    _, pull_in = jax.vjp(norm_apply, resid, gain_in)
    d_from_norm, g_gain_in = pull_in(d_normed)
    d_input = d_hidden1 + d_from_norm
    large_grads = (g_proj[0], g_proj[1], g_proj[2], g_proj[3], g_out)
    small_grads = (g_gain_in, grads[6], grads[7], grads[8], g_proj[4], g_proj[5], grads[9], grads[10], grads[11])
    return (d_input, large_grads, small_grads)

def reference(block_input, segments, cotangent, gain_in, w_query, w_key, w_value, conv_q, conv_k, conv_v, w_decay, w_beta, a_log, dt_bias, w_gate_out, gain_o, w_out, gain_mid, w_ffgate, w_ffup, w_down):
    large = (w_query, w_key, w_value, w_gate_out, w_out, w_ffgate, w_ffup, w_down)
    small = (gain_in, gain_mid, conv_q, conv_k, conv_v, w_decay, w_beta, a_log, dt_bias, gain_o)
    count_seq = TOKENS // SEQ
    per_block = min(count_seq, max(1, 4096 // SEQ))
    blocks = count_seq // per_block
    rows = per_block * SEQ
    xs = block_input.reshape(blocks, rows, block_input.shape[1])
    ss = segments.reshape(blocks, rows)
    cs = cotangent.reshape(blocks, rows, cotangent.shape[1])
    zero_large = tuple((jnp.zeros(item.shape, jnp.float32) for item in large))
    zero_small = tuple((jnp.zeros(item.shape, jnp.float32) for item in small))

    def block_step(carry, item):
        xb, sb, cb = item
        saved, output = forward_pass(xb, sb, large, small)
        d_hidden1, ffn_grads, g_gain_mid = backward_ffn(saved, cb, large, small)
        d_input, mix_grads, mix_small = backward_mixer(saved, d_hidden1, large, small)
        new_large = mix_grads + ffn_grads
        new_small = (mix_small[0], g_gain_mid) + mix_small[1:]
        carry_large = jax.tree.map(jnp.add, carry[0], new_large)
        carry_small = jax.tree.map(jnp.add, carry[1], new_small)
        return ((carry_large, carry_small), (output, d_input))
    (total_large, total_small), (outputs, d_inputs) = lax.scan(block_step, (zero_large, zero_small), (xs, ss, cs))
    block_output = outputs.reshape(block_input.shape)
    d_input = d_inputs.reshape(block_input.shape)
    g_query, g_key, g_value, g_gate_out, g_out, g_ffgate, g_ffup, g_down = total_large
    g_gain_in, g_gain_mid, g_conv_q, g_conv_k, g_conv_v, g_decay, g_beta, g_a_log, g_dt_bias, g_gain_o = total_small
    return (block_output, d_input, g_gain_in, g_query, g_key, g_value, g_conv_q, g_conv_k, g_conv_v, g_decay, g_beta, g_a_log, g_dt_bias, g_gate_out, g_gain_o, g_out, g_gain_mid, g_ffgate, g_ffup, g_down)
```

```python
from functools import partial

import jax
import jax.numpy as jnp
from jax import lax
from jax.experimental import pallas as pl
from jax.experimental.pallas import tpu as pltpu
from jax.sharding import PartitionSpec as P

SEQ = 128
LANES = 128


def dot_plain(left, right):
    return jnp.dot(left, right, preferred_element_type=jnp.float32)


def dot_trans(left, right):
    return lax.dot_general(
        left, right, (((1,), (1,)), ((), ())), preferred_element_type=jnp.float32
    )


def split_two(x):
    high = x.astype(jnp.bfloat16)
    return high, (x - high.astype(jnp.float32)).astype(jnp.bfloat16)


def mm(left, right, dims=((1,), (0,))):
    lh, ll = split_two(left)
    rh, rl = split_two(right)
    dot = partial(
        lax.dot_general, dimension_numbers=(dims, ((), ())), preferred_element_type=jnp.float32
    )
    return dot(lh, rh) + (dot(lh, rl) + dot(ll, rh))


MM_T = ((1,), (1,))
T_MM = ((0,), (0,))


def sigmoid(x):
    return 1.0 / (1.0 + jnp.exp(-x))


def conv_pre(x, taps, masks):
    total = x * taps[0:1]
    for lag in range(1, taps.shape[0]):
        total = total + pltpu.roll(x, lag, 0) * taps[lag : lag + 1] * masks[:, lag : lag + 1]
    return total


def conv_back(x, pre, d_out, taps, masks):
    sig = sigmoid(pre)
    d_pre = d_out * sig * (1.0 + pre * (1.0 - sig))
    rows = x.shape[0]
    d_x = d_pre * taps[0:1]
    d_taps = [jnp.sum(d_pre * x, axis=0, keepdims=True)]
    for lag in range(1, taps.shape[0]):
        part = d_pre * masks[:, lag : lag + 1]
        d_x = d_x + pltpu.roll(part, rows - lag, 0) * taps[lag : lag + 1]
        d_taps.append(jnp.sum(part * pltpu.roll(x, lag, 0), axis=0, keepdims=True))
    return d_x, d_taps


def unit(c):
    scale = lax.rsqrt(jnp.sum(c * c, axis=-1, keepdims=True) + 1e-06)
    return c * scale, scale


def gates(db, rates, bias):
    x = db[:, :LANES] + bias
    soft = jnp.maximum(x, 0.0) + jnp.log1p(jnp.exp(-jnp.abs(x)))
    return x, rates * soft, sigmoid(db[:, LANES:])


def triangle(rows):
    t = lax.broadcasted_iota(jnp.int32, (rows, rows), 0)
    s = lax.broadcasted_iota(jnp.int32, (rows, rows), 1)
    return t, s, (t >= s).astype(jnp.float32)


def sums_to(log_decay, lower):
    down = mm(lower, log_decay)
    across = mm(log_decay, lower, ((0,), (1,)))
    return down, across


def unit_inverse(off, t, s):
    rows = off.shape[0]
    inverse = (t == s).astype(jnp.float32)
    step = 0
    while (1 << step) < rows:
        here = ((t >> (step + 1)) == (s >> (step + 1))) & ((t >> step) != (s >> step))
        part = jnp.where(here, off, 0.0)
        if step == 0:
            inverse = inverse - part
        else:
            inverse = inverse - mm(mm(inverse, part), inverse)
        step += 1
    return inverse


def forward_kernel(
    heads, qp, kp, vp, zp, db, same, masks, conv_q, conv_k, conv_v, rates, bias, gain,
    mixed, inverse_out, fresh_out, core_out,
):
    rows = qp.shape[0]
    wk = qp.shape[1] // heads
    wv = vp.shape[1] // heads
    t, s, lower = triangle(rows)
    _, log_decay, beta = gates(db[...], rates[...], bias[...])
    down, across = sums_to(log_decay, lower)
    masks_v = masks[...]
    same_v = same[...]
    for h in range(heads):
        ks = slice(h * wk, (h + 1) * wk)
        vs = slice(h * wv, (h + 1) * wv)
        pre_q = conv_pre(qp[:, ks], conv_q[:, ks], masks_v)
        pre_k = conv_pre(kp[:, ks], conv_k[:, ks], masks_v)
        pre_v = conv_pre(vp[:, vs], conv_v[:, vs], masks_v)
        q = unit(pre_q * sigmoid(pre_q))[0] * wk ** (-0.5)
        k = unit(pre_k * sigmoid(pre_k))[0]
        v = pre_v * sigmoid(pre_v)
        b = beta[:, h : h + 1]
        decay = jnp.exp(jnp.minimum(down[:, h : h + 1] - across[h : h + 1, :], 0.0)) * same_v
        off = jnp.where(t > s, b * decay * mm(k, k, MM_T), 0.0)
        inverse = unit_inverse(off, t, s)
        fresh = mm(inverse, b * v)
        core = mm(mm(q, k, MM_T) * decay, fresh)
        z = zp[:, vs]
        scale = lax.rsqrt(jnp.mean(core * core, axis=-1, keepdims=True) + 1e-05)
        mixed[:, vs] = (core * scale * gain[...] * (z * sigmoid(z))).astype(mixed.dtype)
        inverse_out[h] = inverse
        fresh_out[:, vs] = fresh
        core_out[:, vs] = core


def backward_kernel(
    heads, qp, kp, vp, zp, db, same, masks, conv_q, conv_k, conv_v, rates, bias, gain,
    inverse_in, fresh_in, core_in, d_mixed,
    dqp, dkp, dvp, dzp, ddb, d_conv_q, d_conv_k, d_conv_v, d_rate, d_bias, d_gain,
):
    rows = qp.shape[0]
    wk = qp.shape[1] // heads
    wv = vp.shape[1] // heads
    t, s, lower = triangle(rows)
    strict = t > s
    x, log_decay, beta = gates(db[...], rates[...], bias[...])
    down, across = sums_to(log_decay, lower)
    masks_v = masks[...]
    same_v = same[...]
    lane = lax.broadcasted_iota(jnp.int32, (rows, LANES), 1)
    line = lax.broadcasted_iota(jnp.int32, (LANES, rows), 0)
    by_row = jnp.zeros((rows, LANES), jnp.float32)
    by_column = jnp.zeros((LANES, rows), jnp.float32)
    d_beta = jnp.zeros((rows, LANES), jnp.float32)
    g_gain = jnp.zeros((1, wv), jnp.float32)
    for h in range(heads):
        ks = slice(h * wk, (h + 1) * wk)
        vs = slice(h * wv, (h + 1) * wv)
        z = zp[:, vs]
        core = core_in[:, vs]
        fresh = fresh_in[:, vs]
        dm = d_mixed[:, vs]
        scale = lax.rsqrt(jnp.mean(core * core, axis=-1, keepdims=True) + 1e-05)
        n = core * scale
        sig = sigmoid(z)
        swish = z * sig
        dmn = dm * n
        dzp[:, vs] = (dmn * gain[...] * sig * (1.0 + z * (1.0 - sig))).astype(dzp.dtype)
        g_gain = g_gain + jnp.sum(dmn * swish, axis=0, keepdims=True)
        dn = dm * gain[...] * swish
        d_core = scale * (dn - n * jnp.mean(dn * n, axis=-1, keepdims=True))
        pre_q = conv_pre(qp[:, ks], conv_q[:, ks], masks_v)
        pre_k = conv_pre(kp[:, ks], conv_k[:, ks], masks_v)
        pre_v = conv_pre(vp[:, vs], conv_v[:, vs], masks_v)
        qn, q_scale = unit(pre_q * sigmoid(pre_q))
        q = qn * wk ** (-0.5)
        k, k_scale = unit(pre_k * sigmoid(pre_k))
        v = pre_v * sigmoid(pre_v)
        b = beta[:, h : h + 1]
        decay = jnp.exp(jnp.minimum(down[:, h : h + 1] - across[h : h + 1, :], 0.0)) * same_v
        inner = jnp.where(strict, decay * mm(k, k, MM_T), 0.0)
        scores = mm(q, k, MM_T) * decay
        d_fresh = mm(scores, d_core, T_MM)
        d_scores = mm(d_core, fresh, MM_T)
        w = mm(inverse_in[h], d_fresh, T_MM)
        d_off = jnp.where(strict, -mm(w, fresh, MM_T), 0.0)
        d_qk = d_scores * decay
        d_kk = d_off * b * decay
        d_inner = d_off * inner
        through = d_scores * scores + d_inner * b
        by_row = by_row + jnp.where(lane == h, jnp.sum(through, axis=1, keepdims=True), 0.0)
        by_column = by_column + jnp.where(line == h, jnp.sum(through, axis=0, keepdims=True), 0.0)
        db_h = jnp.sum(d_inner, axis=1, keepdims=True) + jnp.sum(w * v, axis=1, keepdims=True)
        d_beta = d_beta + jnp.where(lane == h, db_h, 0.0)
        d_q = mm(d_qk, k) * wk ** (-0.5)
        d_k = mm(d_qk, q, T_MM) + mm(d_kk, k) + mm(d_kk, k, T_MM)
        d_cq = q_scale * (d_q - qn * jnp.sum(d_q * qn, axis=-1, keepdims=True))
        d_ck = k_scale * (d_k - k * jnp.sum(d_k * k, axis=-1, keepdims=True))
        for place, source, pre, d_c, taps, d_taps, cols in (
            (dqp, qp, pre_q, d_cq, conv_q, d_conv_q, ks),
            (dkp, kp, pre_k, d_ck, conv_k, d_conv_k, ks),
            (dvp, vp, pre_v, b * w, conv_v, d_conv_v, vs),
        ):
            d_x, parts = conv_back(source[:, cols], pre, d_c, taps[:, cols], masks_v)
            place[:, cols] = d_x.astype(place.dtype)
            for lag, part in enumerate(parts):
                d_taps[lag : lag + 1, cols] = part
    d_log = mm(lower, by_row, T_MM) - mm(lower, by_column, ((0,), (1,)))
    d_x = d_log * rates[...] * sigmoid(x)
    ddb[:, :LANES] = d_x.astype(ddb.dtype)
    ddb[:, LANES:] = (d_beta * beta * (1.0 - beta)).astype(ddb.dtype)
    d_rate[...] = jnp.sum(d_log * log_decay, axis=0, keepdims=True)
    d_bias[...] = jnp.sum(d_x, axis=0, keepdims=True)
    d_gain[...] = g_gain


VMEM = pl.BlockSpec(memory_space=pltpu.VMEM)


def call(kernel, outs, args, flops):
    moved = sum(a.size * a.dtype.itemsize for a in args)
    moved += sum(a.size * a.dtype.itemsize for a in outs)
    return pl.pallas_call(
        kernel,
        out_shape=outs,
        in_specs=[VMEM] * len(args),
        out_specs=tuple(VMEM for _ in outs),
        cost_estimate=pl.CostEstimate(flops=flops, bytes_accessed=moved, transcendentals=0),
        compiler_params=pltpu.CompilerParams(vmem_limit_bytes=48 * 1024 * 1024),
    )(*args)


def shape(dims, dtype=jnp.float32):
    return jax.ShapeDtypeStruct(dims, dtype)


def mixer_forward(heads, args):
    rows = args[0].shape[0]
    wide = args[2].shape[1]
    outs = (
        shape((rows, wide), jnp.bfloat16),
        shape((heads, rows, rows)),
        shape((rows, wide)),
        shape((rows, wide)),
    )
    return call(partial(forward_kernel, heads), outs, args, 4 * 10**9)


def mixer_backward(heads, args, saved, d_mixed):
    qp, kp, vp, zp, db = args[:5]
    outs = tuple(shape(a.shape, jnp.bfloat16) for a in (qp, kp, vp, zp, db))
    outs += tuple(shape(a.shape) for a in args[7:10])
    outs += (shape((1, LANES)), shape((1, LANES)), shape(args[12].shape))
    return call(partial(backward_kernel, heads), outs, args + saved + (d_mixed,), 4 * 10**9)


def swap(array, axis, bit):
    count = lax.axis_size(axis)
    return lax.ppermute(array, axis, [(i, i ^ bit) for i in range(count)])


def two_power(count):
    return count & (count - 1) == 0


def pick(array, index):
    return lax.dynamic_slice_in_dim(array, index, 1, 0)


def gather_weight(weight):
    count = lax.axis_size("shard")
    rows, width = weight.shape
    if count != 4 or lax.axis_size("rep") % 2 or rows % 2:
        return lax.all_gather(weight, "shard", axis=0, tiled=True)
    me = lax.axis_index("shard")
    side = lax.axis_index("rep") % 2
    halves = weight.reshape(2, rows // 2, width)
    far = swap(pick(halves, side), "shard", 2)
    far_other = swap(far, "rep", 1)
    near = swap(halves, "shard", 1)
    cross = swap(far, "shard", 1)
    cross_other = swap(far_other, "shard", 1)
    whole = jnp.zeros((2 * count, rows // 2, width), weight.dtype)
    for piece, place in (
        (halves, 2 * me),
        (near, 2 * (me ^ 1)),
        (far, 2 * (me ^ 2) + side),
        (far_other, 2 * (me ^ 2) + 1 - side),
        (cross, 2 * (me ^ 3) + side),
        (cross_other, 2 * (me ^ 3) + 1 - side),
    ):
        whole = lax.dynamic_update_slice_in_dim(whole, piece, place, 0)
    return whole.reshape(count * rows, width)


def gather_tokens(factor):
    if lax.axis_size("shard") != 4:
        return lax.all_gather(factor, "shard", axis=0, tiled=True)
    far = swap(factor, "shard", 2)
    near = swap(factor, "shard", 1)
    cross = swap(far, "shard", 1)
    return jnp.concatenate([factor, near, far, cross], axis=0)


def own_columns(factor):
    count = lax.axis_size("shard")
    me = lax.axis_index("shard")
    turned = factor.T.reshape(count, factor.shape[1] // count, factor.shape[0])
    if count != 4:
        blocks = lax.all_to_all(turned, "shard", 0, 0, tiled=True)
        return jnp.concatenate([blocks[i] for i in range(count)], axis=1)
    parts = [pick(turned, me)[0]]
    for bit in (1, 2, 3):
        parts.append(swap(pick(turned, me ^ bit), "shard", bit)[0])
    return jnp.concatenate(parts, axis=1)


def sum_over_replicas(turned):
    count = lax.axis_size("rep")
    width, rows = turned.shape
    if not two_power(count):
        done = lax.psum_scatter(turned, "rep", scatter_dimension=0, tiled=True)
        return done.T.astype(jnp.float32)
    bits = count.bit_length() - 1
    me = lax.axis_index("rep")
    held = turned.reshape((2,) * bits + (width // count, rows))
    order = [0] + list(range(bits - 1, 0, -1))
    for step, bit in enumerate(order):
        axis = bits - 1 - bit
        mine = (me >> bit) & 1
        keep = lax.dynamic_slice_in_dim(held, mine, 1, axis)
        sent = lax.dynamic_slice_in_dim(held, 1 - mine, 1, axis)
        got = swap(sent, "rep", 1 << bit)
        held = keep.astype(jnp.float32) + got.astype(jnp.float32)
        if step < bits - 1:
            held = held.astype(turned.dtype)
    return held.reshape(width // count, rows).T


def sum_over_all(array):
    for axis in ("shard", "rep"):
        count = lax.axis_size(axis)
        if two_power(count):
            for bit in range(count.bit_length() - 1):
                array = array + swap(array, axis, 1 << bit)
        else:
            array = lax.psum(array, axis)
    return array


def norm_parts(hidden):
    scale = lax.rsqrt(jnp.mean(hidden * hidden, axis=-1, keepdims=True) + 1e-05)
    return hidden * scale, scale


def norm_back(unit_hidden, scale, gain, d_out):
    d_unit = d_out * gain
    inner = jnp.mean(d_unit * unit_hidden, axis=-1, keepdims=True)
    return scale * (d_unit - unit_hidden * inner), jnp.sum(d_out * unit_hidden, axis=0)


def lanes_of(row):
    return jnp.pad(row, (0, LANES - row.shape[0])).reshape(1, LANES)


def weight_grad(left_own, right):
    return lax.dot_general(
        gather_tokens(right),
        left_own,
        (((0,), (1,)), ((), ())),
        preferred_element_type=jnp.float32,
    ).astype(jnp.bfloat16)


def body(
    block_input,
    segments,
    cotangent,
    gain_in,
    w_query,
    w_key,
    w_value,
    conv_q,
    conv_k,
    conv_v,
    w_decay,
    w_beta,
    a_log,
    dt_bias,
    w_gate_out,
    gain_o,
    w_out,
    gain_mid,
    w_ffgate,
    w_ffup,
    w_down,
):
    heads = a_log.shape[0]
    rows = block_input.shape[0]
    wq, wk, wv, wz, wo, wg, wu, wd = [
        gather_weight(w)
        for w in (w_query, w_key, w_value, w_gate_out, w_out, w_ffgate, w_ffup, w_down)
    ]
    room = LANES - heads
    w_db = jnp.concatenate(
        [jnp.pad(w_decay, ((0, 0), (0, room))), jnp.pad(w_beta, ((0, 0), (0, room)))], axis=1
    )

    resid = block_input.astype(jnp.float32)
    unit_in, scale_in = norm_parts(resid)
    normed = (unit_in * gain_in).astype(jnp.bfloat16)
    qp, kp, vp, zp, db = [dot_plain(normed, w) for w in (wq, wk, wv, wz, w_db)]
    seg = segments.reshape(rows // SEQ, SEQ)
    place = jnp.arange(SEQ)
    same = (
        (seg[:, :, None] == seg[:, None, :]) & (place[:, None] >= place[None, :])
    ).astype(jnp.float32)
    lags = [
        jnp.pad(seg, ((0, 0), (lag, 0)), constant_values=-1)[:, :SEQ] == seg
        for lag in range(conv_q.shape[0])
    ]
    masks = jnp.stack(lags, axis=-1).astype(jnp.float32)
    rates = lanes_of(-jnp.exp(a_log))
    bias = lanes_of(dt_bias)
    gain = gain_o.reshape(1, -1)
    calls = []
    for i in range(rows // SEQ):
        cut = slice(i * SEQ, (i + 1) * SEQ)
        args = (qp[cut], kp[cut], vp[cut], zp[cut], db[cut], same[i], masks[i])
        args += (conv_q, conv_k, conv_v, rates, bias, gain)
        calls.append((args, mixer_forward(heads, args)))
    mixed = jnp.concatenate([out[0] for _, out in calls], axis=0)
    hidden1 = resid + dot_plain(mixed, wo)
    unit_mid, scale_mid = norm_parts(hidden1)
    normed2 = (unit_mid * gain_mid).astype(jnp.bfloat16)
    gate = dot_plain(normed2, wg)
    up = dot_plain(normed2, wu)
    sig = jax.nn.sigmoid(gate)
    act = (gate * sig * up).astype(jnp.bfloat16)
    output = (hidden1 + dot_plain(act, wd)).astype(jnp.bfloat16)

    d_act = dot_trans(cotangent, wd)
    d_gate = (d_act * up * sig * (1.0 + gate * (1.0 - sig))).astype(jnp.bfloat16)
    d_up = (d_act * gate * sig).astype(jnp.bfloat16)
    d_normed2 = dot_trans(d_gate, wg) + dot_trans(d_up, wu)
    d_from_norm, g_gain_mid = norm_back(unit_mid, scale_mid, gain_mid, d_normed2)
    d_hidden1 = cotangent.astype(jnp.float32) + d_from_norm
    normed2_own = own_columns(normed2)
    g_down = sum_over_replicas(weight_grad(own_columns(act), cotangent))
    g_ffgate = sum_over_replicas(weight_grad(normed2_own, d_gate))
    g_ffup = sum_over_replicas(weight_grad(normed2_own, d_up))

    d_hidden_b = d_hidden1.astype(jnp.bfloat16)
    d_mixed = dot_trans(d_hidden_b, wo)
    g_out = sum_over_replicas(weight_grad(own_columns(mixed), d_hidden_b))
    backs = []
    for i, (args, out) in enumerate(calls):
        backs.append(mixer_backward(heads, args, out[1:], d_mixed[i * SEQ : (i + 1) * SEQ]))
    dqp, dkp, dvp, dzp, ddb = [
        jnp.concatenate([back[j] for back in backs], axis=0) for j in range(5)
    ]
    g_conv_q, g_conv_k, g_conv_v, g_rate, g_bias, g_gain_o = [
        sum(back[j] for back in backs) for j in range(5, 11)
    ]
    normed_own = own_columns(normed)
    g_query, g_key, g_value, g_gate_out = [
        sum_over_replicas(weight_grad(normed_own, item)) for item in (dqp, dkp, dvp, dzp)
    ]
    g_db = lax.dot_general(
        ddb, normed, (((0,), (0,)), ((), ())), preferred_element_type=jnp.float32
    )
    g_db = jnp.concatenate([g_db[:heads], g_db[LANES : LANES + heads]], axis=0)
    d_normed = (
        dot_trans(dqp, wq)
        + dot_trans(dkp, wk)
        + dot_trans(dvp, wv)
        + dot_trans(dzp, wz)
        + dot_trans(ddb, w_db)
    )
    d_from_norm, g_gain_in = norm_back(unit_in, scale_in, gain_in, d_normed)
    d_input = d_hidden1 + d_from_norm

    small = (g_gain_in, g_gain_mid, g_conv_q, g_conv_k, g_conv_v, g_db, g_rate, g_bias, g_gain_o)
    flat = jnp.concatenate([item.reshape(-1, LANES) for item in small], axis=0)
    flat = sum_over_all(flat)
    done, start = [], 0
    for item in small:
        stop = start + item.size // LANES
        done.append(flat[start:stop].reshape(item.shape))
        start = stop
    g_gain_in, g_gain_mid, g_conv_q, g_conv_k, g_conv_v, g_db, g_rate, g_bias, g_gain_o = done
    return (
        output,
        d_input,
        g_gain_in,
        g_query,
        g_key,
        g_value,
        g_conv_q,
        g_conv_k,
        g_conv_v,
        g_db[:heads].T,
        g_db[heads:].T,
        g_rate[0, :heads],
        g_bias[0, :heads],
        g_gate_out,
        g_gain_o[0],
        g_out,
        g_gain_mid,
        g_ffgate,
        g_ffup,
        g_down,
    )


def solution(mesh):
    split = P(("shard", "rep"))
    tokens = P(("shard", "rep"), None)
    weight = P("shard", None)
    grad = P("shard", "rep")
    copied = P()
    return jax.shard_map(
        body,
        mesh=mesh,
        in_specs=(
            (tokens, split, tokens, copied)
            + (weight,) * 3
            + (copied,) * 7
            + (weight, copied, weight, copied)
            + (weight,) * 3
        ),
        out_specs=(
            (tokens, tokens, copied)
            + (grad,) * 3
            + (copied,) * 7
            + (grad, copied, grad, copied)
            + (grad,) * 3
        ),
        check_vma=False,
    )
```
